32 devices in a mesh: span: 8 (over z, x), tensor: 4 (over y, core).
Axes of the slice: x: 2, y: 2, z: 4, core: 2. Of those that a mesh axis runs over, the one named last changes fastest.
Arguments:
- latents: bfloat16 [1024, 5120], P(('span', 'tensor')), may hold values from -6 to 6
- modulation: float32 [4, 3, 5120], replicated, may hold values from -3 to 3
- w_query: bfloat16 [5120, 4096], P(None, 'tensor'), may hold values from -0.078125 to 0.078125
- w_key: bfloat16 [5120, 4096], P(None, 'tensor'), may hold values from -0.078125 to 0.078125
- w_value: bfloat16 [5120, 4096], P(None, 'tensor'), may hold values from -0.078125 to 0.078125
- w_out: bfloat16 [4096, 5120], P('tensor'), may hold values from -0.5 to 0.5
- cache_k: bfloat16 [2048, 4096], P('span', 'tensor'), may hold values from -800 to 800
- cache_v: bfloat16 [2048, 4096], P('span', 'tensor'), may hold values from -6 to 6
- level_index: int32 [8], P('span'), may hold values from 0 to 3
- rotation: int32 [8], replicated, may hold values from 0 to 7, each once
- cached_tokens: int32 [1], replicated, may hold values from 128 to 2048
Outputs:
- branch: bfloat16 [1024, 5120], P(('span', 'tensor'))
The draws below stay inside these ranges and needn't reach their ends.
All inputs are finite; a program needn't handle non-finite values.
Results may differ from the reference program's by a relative error of at most 0.019.
Values may be sent and summed in bfloat16 or wider, within the bound.
No kernel may reach another device: no remote copies, remote signals or barrier semaphores. Data moves between devices by JAX's collectives and lax.ppermute only.
A program may use at most 128 MiB of HBM per device.

```python
import jax
import jax.numpy as jnp
from jax import lax

D = 5120
HEADS = 32
HD = 128
LEVELS = 4
SPAN_TOK = 128
TOKENS = 1024
CACHE_TOK = 2048
INNER = 4096
N_SPAN = 8


def draw_cache_k(key, part):
    base = jnp.clip(jax.random.normal(key, (CACHE_TOK, HEADS * HD), jnp.float32), -6.0, 6.0)
    return base.astype(jnp.bfloat16)


def set_ends(entries, key, smallest, top_value):
    longest = entries.shape.index(max(entries.shape))
    spots = []
    for shift in (0, 1):
        where = [jax.random.randint(jax.random.fold_in(key, axis), (), 0, length) for axis, length in enumerate(entries.shape)]
        where[longest] = (where[longest] + shift) % entries.shape[longest]
        spots.append(tuple(where))
    return entries.at[spots[0]].set(smallest).at[spots[1]].set(top_value)


def block_levels(key, extent, shards, smallest, largest):
    def one(position, blocks):
        draws = jax.random.uniform(jax.random.fold_in(jax.random.fold_in(key, 6), position), (blocks,), jnp.float32, smallest / len(shards), largest / len(shards))
        return jnp.repeat(jnp.exp(draws), extent[position] // blocks).reshape((-1,) + (1,) * (len(extent) - position - 1))

    level = one(*shards[0])
    for cut in shards[1:]:
        level = level * one(*cut)
    return level


def noise(rng, dims, spread, bound, shards=(), held_as=jnp.bfloat16):
    array = spread * jax.random.normal(rng, dims, jnp.float32)
    if shards:
        array = array * block_levels(rng, dims, shards, -0.22, 0.18)
    return jnp.clip(array, -bound, bound).astype(held_as)


def setup_inputs(seed: int = 0) -> dict:
    keys = jax.random.split(jax.random.key(seed), 12)
    latents = noise(keys[0], (TOKENS, D), 1.0, 6.0, ((0, 32),))
    modulation = noise(keys[1], (LEVELS, 3, D), 0.5, 3.0, (), jnp.float32)
    w_query = noise(keys[2], (D, INNER), D ** -0.5, 0.078125, ((1, 4),))
    w_key = noise(keys[3], (D, INNER), D ** -0.5, 0.078125, ((1, 4),))
    w_value = noise(keys[4], (D, INNER), D ** -0.5, 0.078125, ((1, 4),))
    w_out = noise(keys[5], (INNER, D), HD ** -0.5, 0.5, ((0, 4),))
    cache_k = draw_cache_k(jax.random.fold_in(keys[11], 71), 0)
    cache_v = noise(keys[7], (CACHE_TOK, INNER), 1.0, 6.0, ((0, 8), (1, 4)))
    level_index = set_ends(jax.random.randint(keys[8], (N_SPAN,), 0, LEVELS), jax.random.fold_in(keys[8], 1), 0, LEVELS - 1).astype(jnp.int32)
    rotation = jax.random.permutation(keys[9], N_SPAN).astype(jnp.int32)
    cached_tokens = jax.random.randint(keys[10], (1,), SPAN_TOK, CACHE_TOK + 1).astype(jnp.int32)
    return dict(latents=latents, modulation=modulation, w_query=w_query, w_key=w_key, w_value=w_value, w_out=w_out, cache_k=cache_k, cache_v=cache_v, level_index=level_index, rotation=rotation, cached_tokens=cached_tokens)


EPSILON = 1e-06

def reference(latents, modulation, w_query, w_key, w_value, w_out, cache_k, cache_v, level_index, rotation, cached_tokens):
    groups = N_SPAN
    mod_rows = jnp.take(modulation, level_index, axis=0)
    row_data = latents.astype(jnp.float32).reshape(groups, SPAN_TOK, D)
    row_mean = lax.optimization_barrier(jnp.mean(row_data, axis=-1, keepdims=True))
    centred = row_data - row_mean
    row_var = lax.optimization_barrier(jnp.mean(centred * centred, axis=-1, keepdims=True))
    normed = centred * lax.rsqrt(row_var + EPSILON)
    modulated = (normed * (1.0 + mod_rows[:, 1:2, :]) + mod_rows[:, 0:1, :]).astype(jnp.bfloat16).reshape(TOKENS, D)
    queries = jnp.dot(modulated, w_query, preferred_element_type=jnp.float32).astype(jnp.bfloat16)
    keys_new = jnp.dot(modulated, w_key, preferred_element_type=jnp.float32).astype(jnp.bfloat16)
    values_new = jnp.dot(modulated, w_value, preferred_element_type=jnp.float32).astype(jnp.bfloat16)
    order = rotation.astype(jnp.int32)
    live_keys = cached_tokens[0]
    cache_valid = jnp.arange(CACHE_TOK, dtype=jnp.int32) < live_keys
    all_keys = jnp.concatenate([cache_k, keys_new], 0).reshape(-1, HEADS, HD).transpose(1, 0, 2)
    all_values = jnp.concatenate([cache_v, values_new], 0).reshape(-1, HEADS, HD).transpose(1, 0, 2)
    key_group = jnp.arange(TOKENS, dtype=jnp.int32) // SPAN_TOK

    def one_span(span):
        allowed = order[key_group] <= order[span]
        key_valid = jnp.concatenate([cache_valid, allowed])
        q_block = lax.dynamic_slice_in_dim(queries, (span * SPAN_TOK).astype(jnp.int32), SPAN_TOK, 0)
        q_block = q_block.reshape(SPAN_TOK, HEADS, HD).transpose(1, 0, 2)

        def one_head(operands):
            q_head, k_head, v_head = operands
            scores = jnp.dot(q_head, k_head.T, preferred_element_type=jnp.float32) * HD ** (-0.5)
            scores = jnp.where(key_valid[None, :], scores, -1e+30)
            top_score = lax.optimization_barrier(jnp.max(scores, axis=1, keepdims=True))
            weights = jnp.where(key_valid[None, :], jnp.exp(scores - top_score), 0.0)
            summed = jnp.dot(weights.astype(jnp.bfloat16), v_head, preferred_element_type=jnp.float32)
            return summed / lax.optimization_barrier(jnp.sum(weights, axis=1, keepdims=True))
        result = lax.map(one_head, (q_block, all_keys, all_values))
        return result.transpose(1, 0, 2).reshape(SPAN_TOK, HEADS * HD).astype(jnp.bfloat16)
    attended = lax.map(one_span, jnp.arange(groups, dtype=jnp.int32)).reshape(TOKENS, HEADS * HD)
    projection = jnp.dot(attended, w_out, preferred_element_type=jnp.float32).reshape(groups, SPAN_TOK, D)
    return (mod_rows[:, 2:3, :] * projection).astype(jnp.bfloat16).reshape(TOKENS, D)
```

```python
import functools

import jax
import jax.numpy as jnp
from jax import lax
from jax.experimental import pallas as pl
from jax.experimental.pallas import tpu as pltpu
from jax.sharding import PartitionSpec as P

HD = 128


EPSILON = 1e-06


def block_update(running, q_heads, key_block, value_block, key_valid):
    run_max, run_sum, run_acc = running
    head_count = q_heads.shape[1]
    head_size = q_heads.shape[2]
    key_heads = key_block.reshape(key_block.shape[0], head_count, head_size)
    value_heads = value_block.reshape(value_block.shape[0], head_count, head_size)
    scores = jnp.einsum(
        "qhd,khd->hqk", q_heads, key_heads, preferred_element_type=jnp.float32
    ) * head_size ** (-0.5)
    scores = jnp.where(key_valid[None, None, :], scores, -1e30)
    new_max = jnp.maximum(run_max, jnp.max(scores, axis=-1))
    weights = jnp.where(key_valid[None, None, :], jnp.exp(scores - new_max[..., None]), 0.0)
    rescale = jnp.exp(run_max - new_max)
    run_sum = run_sum * rescale + jnp.sum(weights, axis=-1)
    run_acc = run_acc * rescale[..., None] + jnp.einsum(
        "hqk,khd->hqd",
        weights.astype(jnp.bfloat16),
        value_heads,
        preferred_element_type=jnp.float32,
    )
    return (new_max, run_sum, run_acc)


def attend(running, q_heads, key_rows, value_rows, key_valid):
    running = block_update(running, q_heads, key_rows, value_rows, key_valid)
    return running


def general_body(
    latents,
    modulation,
    w_query,
    w_key,
    w_value,
    w_out,
    cache_k,
    cache_v,
    level_index,
    rotation,
    cached_tokens,
):
    groups = lax.axis_size("span")
    own_index = lax.axis_index("span")
    chooser = (jnp.arange(modulation.shape[0], dtype=jnp.int32) == level_index[0]).astype(
        jnp.float32
    )
    mod_rows = jnp.sum(chooser[:, None, None] * modulation, axis=0)
    shift_row, scale_row, gate_row = (mod_rows[0], mod_rows[1], mod_rows[2])
    row_data = latents.astype(jnp.float32)
    row_mean = jnp.mean(row_data, axis=-1, keepdims=True)
    centred = row_data - row_mean
    row_var = jnp.mean(centred * centred, axis=-1, keepdims=True)
    normed = centred * lax.rsqrt(row_var + EPSILON)
    modulated = (normed * (1.0 + scale_row) + shift_row).astype(jnp.bfloat16)
    shard_piece = lax.all_gather(modulated, "tensor", axis=0, tiled=True)
    projected = [
        jnp.dot(shard_piece, weight, preferred_element_type=jnp.float32).astype(jnp.bfloat16)
        for weight in (w_query, w_key, w_value)
    ]
    joined = jnp.concatenate(projected, axis=1)
    inner_width = w_query.shape[1]
    own_query = joined[:, :inner_width]
    own_key = joined[:, inner_width : 2 * inner_width]
    own_value = joined[:, 2 * inner_width :]
    head_count = inner_width // HD
    span_rows = own_query.shape[0]
    q_heads = own_query.reshape(span_rows, head_count, HD)
    group_ids = jnp.arange(groups, dtype=jnp.int32)
    order_own = jnp.sum(jnp.where(group_ids == own_index, rotation, 0))
    live_keys = cached_tokens[0]
    initial = (
        jnp.full((head_count, span_rows), -1e30, jnp.float32),
        jnp.zeros((head_count, span_rows), jnp.float32),
        jnp.zeros((head_count, span_rows, HD), jnp.float32),
    )
    all_queries = lax.all_gather(own_query, "span", axis=0, tiled=True)
    cache_rows = cache_k.shape[0]
    local_valid = own_index * cache_rows + jnp.arange(cache_rows, dtype=jnp.int32) < live_keys

    def group_partial(group_queries):
        return attend(initial, group_queries, cache_k, cache_v, local_valid)

    partials = lax.map(group_partial, all_queries.reshape(groups, span_rows, head_count, HD))
    source_max, source_sum, source_acc = lax.all_to_all(
        partials, "span", split_axis=0, concat_axis=0, tiled=True
    )
    best_max = jnp.max(source_max, axis=0)
    rescale = jnp.exp(source_max - best_max)
    running = (
        best_max,
        jnp.sum(source_sum * rescale, axis=0),
        jnp.sum(source_acc * rescale[..., None], axis=0),
    )
    key_rows = lax.all_gather(own_key, "span", axis=0, tiled=True)
    value_rows = lax.all_gather(own_value, "span", axis=0, tiled=True)
    key_index = jnp.arange(key_rows.shape[0], dtype=jnp.int32)
    key_group = key_index // span_rows
    key_order = jnp.sum(
        jnp.where(key_group[:, None] == group_ids[None, :], rotation[None, :], 0), axis=1
    )
    key_valid = key_order <= order_own
    run_max, run_sum, run_acc = attend(running, q_heads, key_rows, value_rows, key_valid)
    attended = (
        (run_acc / run_sum[..., None])
        .transpose(1, 0, 2)
        .reshape(span_rows, inner_width)
        .astype(jnp.bfloat16)
    )
    projection = lax.psum_scatter(
        jnp.dot(attended, w_out, preferred_element_type=jnp.float32).astype(jnp.bfloat16),
        "tensor",
        scatter_dimension=0,
        tiled=True,
    ).astype(jnp.float32)
    return (gate_row[None, :] * projection).astype(jnp.bfloat16)


NEG = -1e30
LOG2E = 1.4426950408889634


def whole(shape):
    return pl.BlockSpec(shape, lambda *_: (0,) * len(shape))


def project_kernel(level_ref, *refs, blocks, weights, chunk):
    x_refs = refs[:blocks]
    mod_ref = refs[blocks]
    w_refs = refs[blocks + 1 : blocks + 1 + weights]
    out_ref = refs[blocks + 1 + weights]
    xn_ref, acc_ref, wbuf, sems = refs[blocks + 2 + weights :]
    slots = wbuf.shape[0]
    depth = w_refs[0].shape[0]
    steps = depth // chunk

    def fetch(weight, step, slot):
        return pltpu.make_async_copy(
            w_refs[weight].at[pl.ds(step * chunk, chunk)], wbuf.at[slot], sems.at[slot]
        )

    total = weights * steps
    for index in range(slots):
        fetch(index // steps, index % steps, index).start()
    rows = x_refs[0].shape[0]
    shift = mod_ref[0, 0:1, :]
    scale = 1.0 + mod_ref[0, 1:2, :]
    for index, x_ref in enumerate(x_refs):
        data = x_ref[...].astype(jnp.float32)
        mean = jnp.sum(data, axis=-1, keepdims=True) * (1.0 / depth)
        centred = data - mean
        var = jnp.sum(centred * centred, axis=-1, keepdims=True) * (1.0 / depth)
        normed = centred * lax.rsqrt(var + EPSILON)
        mixed = (normed * scale + shift).astype(jnp.bfloat16)
        for step in range(steps):
            xn_ref[step, pl.ds(index * rows, rows), :] = mixed[:, step * chunk : (step + 1) * chunk]
    heads = out_ref.shape[0]
    for weight in range(weights):
        acc_ref[...] = jnp.zeros_like(acc_ref)

        def one(step, carry, weight=weight):
            index = weight * steps + step
            slot = lax.rem(index, slots)
            fetch(weight, step, slot).wait()
            acc_ref[...] += jnp.dot(
                xn_ref[step], wbuf[slot], preferred_element_type=jnp.float32
            )
            ahead = index + slots
            for later in range(weight, weights):

                @pl.when((ahead >= later * steps) & (ahead < (later + 1) * steps))
                def _(later=later):
                    fetch(later, ahead - later * steps, slot).start()

            return carry

        lax.fori_loop(0, steps, one, 0)
        for head in range(heads):
            out_ref[head, weight] = acc_ref[:, head * HD : (head + 1) * HD].astype(jnp.bfloat16)


def project(level, blocks, modulation, weight_list, chunk=640, slots=4):
    rows, depth = blocks[0].shape
    span_rows = rows * len(blocks)
    width = weight_list[0].shape[1]
    heads = width // HD
    count = len(weight_list)
    steps = depth // chunk
    return pl.pallas_call(
        functools.partial(
            project_kernel, blocks=len(blocks), weights=count, chunk=chunk
        ),
        grid_spec=pltpu.PrefetchScalarGridSpec(
            num_scalar_prefetch=1,
            grid=(1,),
            in_specs=[whole((rows, depth))] * len(blocks)
            + [pl.BlockSpec((1,) + modulation.shape[1:], lambda i, lv: (lv[0], 0, 0))]
            + [pl.BlockSpec(memory_space=pl.ANY)] * count,
            out_specs=whole((heads, count, span_rows, HD)),
            scratch_shapes=[
                pltpu.VMEM((steps, span_rows, chunk), jnp.bfloat16),
                pltpu.VMEM((span_rows, width), jnp.float32),
                pltpu.VMEM((slots, chunk, width), jnp.bfloat16),
                pltpu.SemaphoreType.DMA((slots,)),
            ],
        ),
        out_shape=jax.ShapeDtypeStruct((heads, count, span_rows, HD), jnp.bfloat16),
        compiler_params=pltpu.CompilerParams(vmem_limit_bytes=24 << 20),
        cost_estimate=pl.CostEstimate(
            flops=2 * span_rows * depth * width * count,
            bytes_accessed=2 * depth * width * count,
            transcendentals=0,
        ),
        name="project",
    )(level, *blocks, modulation, *weight_list)


def attend_kernel(rot_ref, live_ref, qkv_ref, cache_ref, out_ref):
    groups = qkv_ref.shape[0]
    span = pl.program_id(0)
    span_rows = qkv_ref.shape[2]
    cache_rows = cache_ref.shape[0] * cache_ref.shape[2]
    new_rows = groups * span_rows
    q = qkv_ref[span, 0]
    dims = (((1,), (1,)), ((), ()))
    keys = cache_ref[:, 0].reshape(cache_rows, HD)
    s_cache = lax.dot_general(q, keys, dims, preferred_element_type=jnp.float32)
    place = lax.broadcasted_iota(jnp.int32, (1, cache_rows), 1)
    s_cache = s_cache + jnp.where(place < live_ref[0], 0.0, NEG)
    s_new = lax.dot_general(
        q, qkv_ref[:, 1].reshape(new_rows, HD), dims, preferred_element_type=jnp.float32
    )
    own = rot_ref[span]
    bias = jnp.concatenate(
        [
            jnp.full((1, span_rows), jnp.where(rot_ref[other] <= own, 0.0, NEG), jnp.float32)
            for other in range(groups)
        ],
        axis=1,
    )
    s_new = s_new + bias
    top = jnp.maximum(
        jnp.max(s_cache, axis=1, keepdims=True), jnp.max(s_new, axis=1, keepdims=True)
    )
    factor = HD**-0.5 * LOG2E
    p_cache = jnp.exp2((s_cache - top) * factor)
    p_new = jnp.exp2((s_new - top) * factor)
    total = jnp.sum(p_cache, axis=1, keepdims=True) + jnp.sum(p_new, axis=1, keepdims=True)
    acc = jnp.dot(
        p_cache.astype(jnp.bfloat16),
        cache_ref[:, 1].reshape(cache_rows, HD),
        preferred_element_type=jnp.float32,
    ) + jnp.dot(
        p_new.astype(jnp.bfloat16),
        qkv_ref[:, 2].reshape(new_rows, HD),
        preferred_element_type=jnp.float32,
    )
    out_ref[0] = (acc / total).astype(jnp.bfloat16)


def attend_all(rotation, live, qkv, cache):
    groups, _, span_rows, _ = qkv.shape
    cache_rows = cache.shape[0] * cache.shape[2]
    keys = cache_rows + groups * span_rows
    return pl.pallas_call(
        attend_kernel,
        grid_spec=pltpu.PrefetchScalarGridSpec(
            num_scalar_prefetch=2,
            grid=(groups,),
            in_specs=[whole(qkv.shape), whole(cache.shape)],
            out_specs=pl.BlockSpec((1, span_rows, HD), lambda g, *_: (g, 0, 0)),
        ),
        out_shape=jax.ShapeDtypeStruct((groups, span_rows, HD), jnp.bfloat16),
        compiler_params=pltpu.CompilerParams(vmem_limit_bytes=32 << 20),
        cost_estimate=pl.CostEstimate(
            flops=4 * groups * span_rows * keys * HD,
            bytes_accessed=2 * (qkv.size + cache.size),
            transcendentals=groups * span_rows * keys,
        ),
        name="attend",
    )(rotation, live, qkv, cache)


def out_kernel(o_ref, w_ref, keep_ref, send_ref):
    heads, span_rows, _ = o_ref.shape
    lhs = jnp.concatenate([o_ref[head] for head in range(heads)], axis=1)
    result = jnp.dot(lhs, w_ref[...], preferred_element_type=jnp.float32)
    half, rows, _ = keep_ref.shape
    for index in range(half):
        keep_ref[index] = result[2 * index * rows : (2 * index + 1) * rows]
        send_ref[index] = result[(2 * index + 1) * rows : (2 * index + 2) * rows].astype(
            jnp.bfloat16
        )


def out_project(attended, w_out, blocks, chunk=640):
    heads, span_rows, _ = attended.shape
    width = w_out.shape[1]
    rows = span_rows // blocks
    half = blocks // 2
    spec = pl.BlockSpec((half, rows, chunk), lambda j: (0, 0, j))
    return pl.pallas_call(
        out_kernel,
        grid=(width // chunk,),
        in_specs=[
            whole(attended.shape),
            pl.BlockSpec((heads * HD, chunk), lambda j: (0, j)),
        ],
        out_specs=[spec, spec],
        out_shape=[
            jax.ShapeDtypeStruct((half, rows, width), jnp.float32),
            jax.ShapeDtypeStruct((half, rows, width), jnp.bfloat16),
        ],
        compiler_params=pltpu.CompilerParams(vmem_limit_bytes=24 << 20),
        cost_estimate=pl.CostEstimate(
            flops=2 * span_rows * heads * HD * width,
            bytes_accessed=2 * heads * HD * width,
            transcendentals=0,
        ),
        name="out_project",
    )(attended, w_out)


def swap(value, bit, size):
    return lax.ppermute(value, "tensor", [(place, place ^ bit) for place in range(size)])


def fast_body(
    latents,
    modulation,
    w_query,
    w_key,
    w_value,
    w_out,
    cache_k,
    cache_v,
    level_index,
    rotation,
    cached_tokens,
):
    groups = lax.axis_size("span")
    tensor = lax.axis_size("tensor")
    cache_rows = cache_k.shape[0]
    packed = jnp.stack(
        [part.reshape(cache_rows, groups, HD).transpose(1, 0, 2) for part in (cache_k, cache_v)],
        axis=1,
    )
    cache = lax.all_to_all(packed, "span", split_axis=0, concat_axis=0, tiled=True)
    blocks = [latents]
    bit = tensor // 2
    order = [0]
    while bit:
        blocks = blocks + [swap(block, bit, tensor) for block in blocks]
        order = order + [place ^ bit for place in order]
        bit //= 2
    blocks = [blocks[order.index(place)] for place in range(tensor)]
    qkv = project(level_index, blocks, modulation, [w_query, w_key, w_value])
    qkv = lax.all_to_all(qkv, "span", split_axis=0, concat_axis=0, tiled=True)
    attended = attend_all(rotation, cached_tokens, qkv, cache)
    attended = lax.all_to_all(attended, "span", split_axis=0, concat_axis=0, tiled=True)
    keep, send = out_project(attended, w_out, tensor)
    parts = [None] * (tensor // 2)
    for index in reversed(range(tensor // 2)):
        parts[index] = keep[index] + swap(send[index], 1, tensor).astype(jnp.float32)
    bit = 2
    while bit < tensor:
        stay, go = parts[0::2], parts[1::2]
        parts = [
            mine + swap(other.astype(jnp.bfloat16), bit, tensor).astype(jnp.float32)
            for mine, other in zip(stay, go)
        ]
        bit *= 2
    gate = lax.dynamic_slice_in_dim(modulation[:, 2, :], level_index[0], 1, axis=0)
    return (gate * parts[0]).astype(jnp.bfloat16)


def solution(mesh):
    placed = (
        P(("span", "tensor"), None),
        P(),
        P(None, "tensor"),
        P(None, "tensor"),
        P(None, "tensor"),
        P("tensor", None),
        P("span", "tensor"),
        P("span", "tensor"),
        P("span"),
        P(),
        P(),
    )

    def body(*args):
        groups = mesh.shape["span"]
        tensor = mesh.shape["tensor"]
        heads = args[2].shape[1] // HD
        if heads == groups and tensor >= 2 and tensor & (tensor - 1) == 0:
            return fast_body(*args)
        return general_body(*args)

    return jax.shard_map(
        body, mesh=mesh, in_specs=placed, out_specs=P(("span", "tensor"), None), check_vma=False
    )
```
